1024 devices in a mesh: seq: 64 (over x_lo, z, core), chan: 16 (over y, x_hi).
Axes of the slice: x: 8 (x_hi: 2, x_lo: 4; x = x_hi * 4 + x_lo), y: 8, z: 8, core: 2. Of those that a mesh axis runs over, the one named last changes fastest.
Arguments:
- q_one: bfloat16 [8192, 8192], P('chan', 'seq'), may hold values from -6 to 6
- k_one: bfloat16 [8192, 8192], P('chan', 'seq'), may hold values from -6 to 6
- v_one: bfloat16 [8192, 8192], P('chan', 'seq'), may hold values from -6 to 6
- fir_taps: bfloat16 [8192, 128], P('chan'), may hold values from -0.5 to 0.5
- q_two: bfloat16 [8192, 8192], P('chan', 'seq'), may hold values from -6 to 6
- k_two: bfloat16 [8192, 8192], P('chan', 'seq'), may hold values from -6 to 6
- residues: float32 [8192, 16], P('chan'), may hold values from -0.0625 to 0.0625
- decays: float32 [8192, 16], P('chan'), may hold values from 3.0517578e-05 to 0.08
- skip_gain: float32 [8192], P('chan'), may hold values from 0.5 to 1.5
Outputs:
- layer_one: bfloat16 [8192, 8192], P('chan', 'seq')
- layer_two: bfloat16 [8192, 8192], P('chan', 'seq')
The draws below stay inside these ranges and needn't reach their ends.
All inputs are finite; a program needn't handle non-finite values.
Results may differ from the reference program's by a relative error of at most 0.012.
Values may be sent and summed in bfloat16 or wider, within the bound.
No kernel may reach another device: no remote copies, remote signals or barrier semaphores. Data moves between devices by JAX's collectives and lax.ppermute only.
A program may use at most 32 MiB of HBM per device.

```python
import math
import jax
import jax.numpy as jnp
from jax import lax

D = 8192
TAPS = 128
MODES = 16
TOKENS = 8192


def block_levels(rng, dims, split, least, largest):
    level = 1.0
    for axis_at, blocks in split:
        draws = jax.random.uniform(jax.random.fold_in(jax.random.fold_in(rng, 6), axis_at), (blocks,), jnp.float32, least / len(split), largest / len(split))
        level = level * jnp.repeat(jnp.exp(draws), dims[axis_at] // blocks).reshape((-1,) + (1,) * (len(dims) - 1 - axis_at))
    return level


def centred(key, extent, width, bound, cuts=(), held_as=jnp.bfloat16):
    gain = block_levels(key, extent, cuts, -0.22, 0.18) if cuts else 1.0
    values = jax.random.normal(key, extent, jnp.float32) * width * gain
    return jnp.minimum(jnp.maximum(values, -bound), bound).astype(held_as)


def setup_inputs(seed: int = 0) -> dict:
    streams_of = jax.random.split(jax.random.key(seed), 10)
    q_one = centred(streams_of[0], (D, TOKENS), 1.0, 6.0, ((0, 16), (1, 64)))
    k_one = centred(streams_of[1], (D, TOKENS), 1.0, 6.0, ((0, 16), (1, 64)))
    v_one = centred(streams_of[2], (D, TOKENS), 1.0, 6.0, ((0, 16), (1, 64)))
    fir_taps = centred(streams_of[3], (D, TAPS), TAPS ** -0.5, 0.5, ((0, 16),))
    q_two = centred(streams_of[4], (D, TOKENS), 1.0, 6.0, ((0, 16), (1, 64)))
    k_two = centred(streams_of[5], (D, TOKENS), 1.0, 6.0, ((0, 16), (1, 64)))
    residues = centred(streams_of[6], (D, MODES), TOKENS ** -0.5, 0.0625, ((0, 16),), jnp.float32)
    decays = jnp.clip(jnp.exp(math.log(0.08) - 7.871479 * jax.random.uniform(streams_of[7], (D, MODES), jnp.float32) ** block_levels(streams_of[7], (D, MODES), ((0, 16),), -0.2, 0.2)), 3.0517578125e-05, 0.08)
    skip_gain = jnp.clip(0.5 + 1.0 * jax.random.uniform(streams_of[8], (D,), jnp.float32) ** block_levels(streams_of[8], (D,), ((0, 16),), -0.2, 0.2), 0.5, 1.5)
    return {"q_one": q_one, "k_one": k_one, "v_one": v_one, "fir_taps": fir_taps, "q_two": q_two, "k_two": k_two, "residues": residues, "decays": decays, "skip_gain": skip_gain}


def causal_filter(signal, fir_kernel):
    kernel = fir_kernel[:, ::-1][:, None, :]
    result = lax.conv_general_dilated(signal[None], kernel, (1,), "VALID", dimension_numbers=("NCH", "OIH", "NCH"), feature_group_count=signal.shape[0], preferred_element_type=jnp.float32)
    return result[0]


def one_block(items):
    q_first, k_first, v_first, fir_kernel, q_second, k_second, mode_res, mode_dec, gain_block = items
    product = (k_first.astype(jnp.float32) * v_first.astype(jnp.float32)).astype(jnp.bfloat16)
    padded = jnp.pad(product, ((0, 0), (TAPS - 1, 0)))
    filtered = causal_filter(padded, fir_kernel)
    first_out = (q_first.astype(jnp.float32) * filtered).astype(jnp.bfloat16)
    mixed_in = (k_second.astype(jnp.float32) * first_out.astype(jnp.float32)).astype(jnp.bfloat16)
    time_axis = jnp.arange(TOKENS, dtype=jnp.float32)
    long_filter = jnp.zeros((mixed_in.shape[0], TOKENS), jnp.float32)
    for mode_index in range(MODES):
        long_filter = long_filter + mode_res[:, mode_index, None] * jnp.exp(-mode_dec[:, mode_index, None] * time_axis[None, :])
    spectrum = jnp.fft.rfft(mixed_in.astype(jnp.float32), n=2 * TOKENS) * jnp.fft.rfft(long_filter, n=2 * TOKENS)
    convolved = jnp.fft.irfft(spectrum, n=2 * TOKENS)[:, :TOKENS]
    rounded = lax.optimization_barrier(convolved.astype(jnp.bfloat16)).astype(jnp.float32)
    second_out = q_second.astype(jnp.float32) * (rounded + gain_block[:, None] * mixed_in.astype(jnp.float32))
    return first_out, second_out.astype(jnp.bfloat16)


def reference(q_one, k_one, v_one, fir_taps, q_two, k_two, residues, decays, skip_gain):
    block = min(D, 256)
    count = D // block
    stacked = (q_one.reshape(count, block, TOKENS), k_one.reshape(count, block, TOKENS), v_one.reshape(count, block, TOKENS), fir_taps.reshape(count, block, TAPS), q_two.reshape(count, block, TOKENS), k_two.reshape(count, block, TOKENS), residues.reshape(count, block, MODES), decays.reshape(count, block, MODES), skip_gain.reshape(count, block))
    first_all, second_all = lax.map(one_block, stacked)
    return first_all.reshape(D, TOKENS), second_all.reshape(D, TOKENS)
```

```python
import jax
import jax.numpy as jnp
from jax import lax
from jax.experimental import pallas as pl
from jax.experimental.pallas import tpu as pltpu
from jax.sharding import Mesh, PartitionSpec as P

LANES = 128
ROWS = 8
F32 = jnp.float32
BF16 = jnp.bfloat16
NEAR = 8


def call(kernel, outs, scratch=()):
    return pl.pallas_call(kernel, out_shape=outs, scratch_shapes=list(scratch))


def array(dtype, *shape):
    return jax.ShapeDtypeStruct(shape, dtype)


def turned(block):
    return jnp.swapaxes(block.astype(F32), 0, 1)


def rows_of(ref, tile, first, count=ROWS):
    return ref[tile, pl.ds(first, count), :]


def spread(ref, tile, row):
    return jnp.broadcast_to(ref[tile, pl.ds(row, 1), :], (ROWS, LANES))


def product_kernel(k_ref, v_ref, out_ref):
    for tile in range(out_ref.shape[0]):
        part = pl.ds(tile * LANES, LANES)
        product = (k_ref[part, :].astype(F32) * v_ref[part, :].astype(F32)).astype(BF16)
        out_ref[tile] = turned(product).astype(BF16)


def own_taps(signal_ref, taps_ref, tile, blocks):
    sums = [jnp.zeros((ROWS, LANES), F32) for _ in range(blocks)]
    for offset in range(ROWS):
        shifted = [rows_of(signal_ref, tile, ROWS + ROWS * at - offset) for at in range(blocks)]
        for step in range(blocks):
            weight = spread(taps_ref, tile, ROWS * step + offset)
            for at in range(step, blocks):
                sums[at] = sums[at] + weight * shifted[at - step]
    return sums


def earlier_taps(sums, signal_ref, taps_ref, tile, blocks):
    sums = list(sums)
    for offset in range(ROWS):
        shifted = {
            at: rows_of(signal_ref, tile, ROWS * (blocks + at) - offset)
            for at in range(1 - blocks, 1 if offset else 0)
        }
        for step in range(blocks):
            weight = spread(taps_ref, tile, ROWS * step + offset)
            for at in range(blocks):
                if at - step in shifted:
                    sums[at] = sums[at] + weight * shifted[at - step]
    return sums


def decayed_sums(starts, decay, blocks):
    out = []
    for at in range(blocks):
        terms = list(starts)
        while len(terms) > 1:
            terms = [a + b for a, b in zip(terms[::2], terms[1::2])]
        out.append(terms[0])
        if at + 1 < blocks:
            starts = [a * b for a, b in zip(starts, decay)]
    return out


def prepare_kernel(
    product_ref, taps_ref, q_ref, k_ref, res_ref, dec_ref,
    taps_out, part_out, q_out, k_out, filter_out, mode_out,
    signal_ref,
):
    tiles, length = product_ref.shape[0], product_ref.shape[1]
    blocks = length // ROWS
    modes = res_ref.shape[1]
    signal_ref[:, pl.ds(0, ROWS), :] = jnp.zeros((tiles, ROWS, LANES), F32)
    for tile in range(tiles):
        part = pl.ds(tile * LANES, LANES)
        signal_ref[tile, pl.ds(ROWS, length), :] = product_ref[tile].astype(F32)
        taps_out[tile] = turned(taps_ref[part, :])
        q_out[tile] = turned(q_ref[part, :])
        k_out[tile] = turned(k_ref[part, :])
        mode_out[tile, pl.ds(0, modes), :] = jnp.swapaxes(res_ref[part, :], 0, 1)
        mode_out[tile, pl.ds(modes, modes), :] = jnp.swapaxes(dec_ref[part, :], 0, 1)

    place = lax.broadcasted_iota(jnp.int32, (ROWS, LANES), 0).astype(F32)

    def one_tile(tile, carry):
        sums = own_taps(signal_ref, taps_out, tile, blocks)
        for at in range(blocks):
            part_out[tile, pl.ds(ROWS * at, ROWS), :] = sums[at]
        starts, decay = [], []
        for mode in range(modes):
            rate = spread(mode_out, tile, modes + mode)
            starts.append(spread(mode_out, tile, mode) * jnp.exp(-rate * place))
            decay.append(jnp.exp(-rate * float(ROWS)))
        for at, value in enumerate(decayed_sums(starts, decay, blocks)):
            filter_out[tile, pl.ds(ROWS * at, ROWS), :] = value
        return carry

    lax.fori_loop(0, tiles, one_tile, 0)


def mix_kernel(
    halo_ref, part_ref, taps_ref, q_ref, k_ref, mode_ref,
    one_out, mixed_out, state_out,
    signal_ref,
):
    tiles, length = part_ref.shape[0], part_ref.shape[1]
    blocks = length // ROWS
    modes = mode_ref.shape[1] // 2
    signal_ref[:, pl.ds(length, ROWS), :] = jnp.zeros((tiles, ROWS, LANES), F32)
    for tile in range(tiles):
        signal_ref[tile, pl.ds(0, length), :] = halo_ref[tile].astype(F32)

    left = (ROWS - 1 - lax.broadcasted_iota(jnp.int32, (ROWS, LANES), 0)).astype(F32)

    def one_tile(tile, carry):
        sums = [rows_of(part_ref, tile, ROWS * at) for at in range(blocks)]
        sums = earlier_taps(sums, signal_ref, taps_ref, tile, blocks)
        mixed = []
        for at in range(blocks):
            rows = pl.ds(ROWS * at, ROWS)
            first = (q_ref[tile, rows, :] * sums[at]).astype(BF16).astype(F32)
            mixed.append((k_ref[tile, rows, :] * first).astype(BF16).astype(F32))
            one_out[tile, rows, :] = first
            mixed_out[tile, rows, :] = mixed[-1]
        found = []
        for mode in range(modes):
            rate = spread(mode_ref, tile, modes + mode)
            decay = jnp.exp(-rate * float(ROWS))
            held = mixed[0]
            for at in range(1, blocks):
                held = held * decay + mixed[at]
            found.append(jnp.sum(held * jnp.exp(-rate * left), axis=0, keepdims=True))
        state = jnp.concatenate(found, axis=0).astype(BF16)
        for peer in range(NEAR):
            state_out[peer, pl.ds(pl.multiple_of(tile * modes, modes), modes), :] = state
        return carry

    lax.fori_loop(0, tiles, one_tile, 0)


def local_kernel(mixed_ref, filter_ref, one_ref, conv_out, one_out, signal_ref):
    tiles, length = mixed_ref.shape[0], mixed_ref.shape[1]
    blocks = length // ROWS
    signal_ref[:, pl.ds(0, ROWS), :] = jnp.zeros((tiles, ROWS, LANES), F32)
    for tile in range(tiles):
        signal_ref[tile, pl.ds(ROWS, length), :] = mixed_ref[tile]
        one_out[pl.ds(tile * LANES, LANES), :] = turned(one_ref[tile]).astype(BF16)

    def one_tile(tile, carry):
        sums = own_taps(signal_ref, filter_ref, tile, blocks)
        for at in range(blocks):
            conv_out[tile, pl.ds(ROWS * at, ROWS), :] = sums[at]
        return carry

    lax.fori_loop(0, tiles, one_tile, 0)


def near_kernel(heard_ref, mode_ref, before_out, whole_out):
    tiles, modes = mode_ref.shape[0], mode_ref.shape[1] // 2
    length = float(LANES)
    me = lax.axis_index("near")
    for tile in range(tiles):
        part = pl.ds(tile * modes, modes)
        step = jnp.exp(-mode_ref[tile, pl.ds(modes, modes), :] * length)
        before = jnp.zeros((modes, LANES), F32)
        whole = jnp.zeros((modes, LANES), F32)
        for peer in range(NEAR):
            state = heard_ref[peer, part, :].astype(F32)
            whole = whole * step + state
            before = jnp.where(peer < me, whole, before)
        before_out[part, :] = before
        for peer in range(whole_out.shape[0]):
            whole_out[peer, part, :] = whole.astype(BF16)


def finish_kernel(heard_ref, before_ref, mode_ref, conv_ref, mixed_ref, gate_ref, gain_ref, out_ref):
    tiles, length = mixed_ref.shape[0], mixed_ref.shape[1]
    blocks = length // ROWS
    modes = mode_ref.shape[1] // 2
    me, group = lax.axis_index("near"), lax.axis_index("far")
    skipped = (me * length).astype(F32)
    after = (1 + lax.broadcasted_iota(jnp.int32, (ROWS, LANES), 0)).astype(F32)
    for tile in range(tiles):
        part = pl.ds(tile * modes, modes)
        rates = mode_ref[tile, pl.ds(modes, modes), :]
        step = jnp.exp(-rates * float(length * NEAR))
        far = jnp.zeros((modes, LANES), F32)
        for peer in range(heard_ref.shape[0] - 1):
            far = jnp.where(peer < group, far * step + heard_ref[peer, part, :].astype(F32), far)
        entering = (before_ref[part, :] + far * jnp.exp(-rates * skipped)) * mode_ref[tile, pl.ds(0, modes), :]
        starts, decay = [], []
        for mode in range(modes):
            rate = jnp.broadcast_to(rates[mode : mode + 1, :], (ROWS, LANES))
            starts.append(jnp.broadcast_to(entering[mode : mode + 1, :], (ROWS, LANES)) * jnp.exp(-rate * after))
            decay.append(jnp.exp(-rate * float(ROWS)))
        gain = jnp.broadcast_to(gain_ref[pl.ds(tile, 1), :], (ROWS, LANES))
        made = []
        for at, value in enumerate(decayed_sums(starts, decay, blocks)):
            rows = pl.ds(ROWS * at, ROWS)
            convolved = (conv_ref[tile, rows, :] + value).astype(BF16).astype(F32)
            made.append(convolved + gain * mixed_ref[tile, rows, :])
        channels = pl.ds(tile * LANES, LANES)
        summed = turned(jnp.concatenate(made, axis=0))
        out_ref[channels, :] = (gate_ref[channels, :].astype(F32) * summed).astype(BF16)


def body(q_one, k_one, v_one, fir_taps, q_two, k_two, residues, decays, skip_gain):
    channels, length = q_one.shape
    tiles, modes = channels // LANES, residues.shape[1]
    seq = ("far", "near")
    far_count = lax.axis_size("far")
    count = far_count * lax.axis_size("near")
    product = call(product_kernel, array(BF16, tiles, length, LANES))(k_one, v_one)
    halo = lax.ppermute(product, seq, [(at, at + 1) for at in range(count - 1)])
    wide = array(F32, tiles, length, LANES)
    padded = pltpu.VMEM((tiles, length + ROWS, LANES), F32)
    taps, part, q_turned, k_turned, long_taps, mode_rows = call(
        prepare_kernel,
        (wide, wide, wide, wide, wide, array(F32, tiles, 2 * modes, LANES)),
        (padded,),
    )(product, fir_taps, q_one, k_two, residues, decays)
    one_turned, mixed, state = call(
        mix_kernel,
        (wide, wide, array(BF16, NEAR, tiles * modes, LANES)),
        (padded,),
    )(halo, part, taps, q_turned, k_turned, mode_rows)
    heard = lax.all_to_all(state, "near", split_axis=0, concat_axis=0, tiled=True)
    conv, layer_one = call(
        local_kernel, (wide, array(BF16, channels, length)), (padded,)
    )(mixed, long_taps, one_turned)
    before, whole = call(
        near_kernel,
        (array(F32, tiles * modes, LANES), array(BF16, far_count, tiles * modes, LANES)),
    )(heard, mode_rows)
    far_heard = lax.all_to_all(whole, "far", split_axis=0, concat_axis=0, tiled=True)
    layer_two = call(finish_kernel, array(BF16, channels, length))(
        far_heard, before, mode_rows, conv, mixed, q_two, skip_gain.reshape(tiles, LANES)
    )
    return (layer_one, layer_two)


def solution(mesh):
    count, chans = mesh.shape["seq"], mesh.shape["chan"]
    grid = Mesh(mesh.devices.reshape(count // NEAR, NEAR, chans), ("far", "near", "chan"))
    split = P("chan", ("far", "near"))
    whole = P("chan", None)
    return jax.shard_map(
        body,
        mesh=grid,
        in_specs=(split, split, split, whole, split, split, whole, whole, P("chan")),
        out_specs=(split, split),
        check_vma=False,
    )
```

```python
import jax
import jax.numpy as jnp
from jax import lax
from jax.experimental import pallas as pl
from jax.experimental.pallas import tpu as pltpu
from jax.sharding import Mesh, PartitionSpec as P

LANES = 128
ROWS = 8
F32 = jnp.float32
BF16 = jnp.bfloat16
LINE = 4
CORES = 2


def call(kernel, outs, scratch=()):
    return pl.pallas_call(kernel, out_shape=outs, scratch_shapes=list(scratch))


def near_by(*args):
    return [pltpu.with_memory_space_constraint(arg, pltpu.VMEM) for arg in args]


def array(dtype, *shape):
    return pltpu.VMEM(shape, dtype)


def turned(block):
    return jnp.swapaxes(block.astype(F32), 0, 1)


def rows_of(ref, tile, first, count=ROWS):
    return ref[tile, pl.ds(first, count), :]


def spread(ref, tile, row):
    return jnp.broadcast_to(ref[tile, pl.ds(row, 1), :], (ROWS, LANES))


def product_kernel(k_ref, v_ref, res_ref, dec_ref, gain_ref, out_ref, mode_out):
    modes = res_ref.shape[0]
    for tile in range(out_ref.shape[0]):
        part = pl.ds(tile * LANES, LANES)
        product = (k_ref[part, :].astype(F32) * v_ref[part, :].astype(F32)).astype(BF16)
        out_ref[tile] = turned(product).astype(BF16)
        mode_out[tile, pl.ds(0, modes), :] = res_ref[:, part]
        mode_out[tile, pl.ds(modes, modes), :] = dec_ref[:, part]
        mode_out[tile, pl.ds(2 * modes, 1), :] = gain_ref[pl.ds(tile, 1), :]


def own_taps(signal_ref, taps_ref, tile, blocks):
    sums = [jnp.zeros((ROWS, LANES), F32) for _ in range(blocks)]
    for offset in range(ROWS):
        shifted = [rows_of(signal_ref, tile, ROWS + ROWS * at - offset) for at in range(blocks)]
        for step in range(blocks):
            weight = spread(taps_ref, tile, ROWS * step + offset)
            for at in range(step, blocks):
                sums[at] = sums[at] + weight * shifted[at - step]
    return sums


def earlier_taps(sums, signal_ref, taps_ref, tile, blocks):
    sums = list(sums)
    for offset in range(ROWS):
        shifted = {
            at: rows_of(signal_ref, tile, ROWS * (blocks + at) - offset)
            for at in range(1 - blocks, 1 if offset else 0)
        }
        for step in range(blocks):
            weight = spread(taps_ref, tile, ROWS * step + offset)
            for at in range(blocks):
                if at - step in shifted:
                    sums[at] = sums[at] + weight * shifted[at - step]
    return sums


def decayed_sums(starts, decay, blocks):
    out = []
    for at in range(blocks):
        terms = list(starts)
        while len(terms) > 1:
            terms = [a + b for a, b in zip(terms[::2], terms[1::2])]
        out.append(terms[0])
        if at + 1 < blocks:
            starts = [a * b for a, b in zip(starts, decay)]
    return out


def own_filter_kernel(product_ref, taps_ref, taps_out, part_out, signal_ref):
    tiles, length = product_ref.shape[0], product_ref.shape[1]
    blocks = length // ROWS
    signal_ref[:, pl.ds(0, ROWS), :] = jnp.zeros((tiles, ROWS, LANES), F32)
    for tile in range(tiles):
        signal_ref[tile, pl.ds(ROWS, length), :] = product_ref[tile].astype(F32)
        taps_out[tile] = turned(taps_ref[pl.ds(tile * LANES, LANES), :])

    def one_tile(tile, carry):
        sums = own_taps(signal_ref, taps_out, tile, blocks)
        for at in range(blocks):
            part_out[tile, pl.ds(ROWS * at, ROWS), :] = sums[at]
        return carry

    lax.fori_loop(0, tiles, one_tile, 0)


def turn_kernel(q_ref, k_ref, q_out, k_out):
    for tile in range(q_out.shape[0]):
        part = pl.ds(tile * LANES, LANES)
        q_out[tile] = turned(q_ref[part, :])
        k_out[tile] = turned(k_ref[part, :])


def mix_kernel(
    halo_ref, part_ref, taps_ref, q_ref, k_ref, mode_ref,
    one_out, mixed_out, state_out,
    signal_ref,
):
    tiles, length = part_ref.shape[0], part_ref.shape[1]
    blocks = length // ROWS
    modes = state_out.shape[1] // tiles
    signal_ref[:, pl.ds(length, ROWS), :] = jnp.zeros((tiles, ROWS, LANES), F32)
    for tile in range(tiles):
        signal_ref[tile, pl.ds(0, length), :] = halo_ref[tile].astype(F32)

    left = (ROWS - 1 - lax.broadcasted_iota(jnp.int32, (ROWS, LANES), 0)).astype(F32)

    def one_tile(tile, carry):
        sums = [rows_of(part_ref, tile, ROWS * at) for at in range(blocks)]
        sums = earlier_taps(sums, signal_ref, taps_ref, tile, blocks)
        mixed = []
        for at in range(blocks):
            rows = pl.ds(ROWS * at, ROWS)
            first = (q_ref[tile, rows, :] * sums[at]).astype(BF16).astype(F32)
            mixed.append((k_ref[tile, rows, :] * first).astype(BF16).astype(F32))
            one_out[tile, rows, :] = first
            mixed_out[tile, rows, :] = mixed[-1]
        found = []
        for mode in range(modes):
            rate = spread(mode_ref, tile, modes + mode)
            decay = jnp.exp(-rate * float(ROWS))
            held = mixed[0]
            for at in range(1, blocks):
                held = held * decay + mixed[at]
            found.append(jnp.sum(held * jnp.exp(-rate * left), axis=0, keepdims=True))
        state = jnp.concatenate(found, axis=0).astype(BF16)
        for peer in range(state_out.shape[0]):
            state_out[peer, pl.ds(pl.multiple_of(tile * modes, modes), modes), :] = state
        return carry

    lax.fori_loop(0, tiles, one_tile, 0)


def local_conv(first, count, mixed_ref, mode_ref, conv_out, signal_ref, filter_ref):
    length = mixed_ref.shape[1]
    blocks = length // ROWS
    modes = (mode_ref.shape[1] - ROWS) // 2
    place = lax.broadcasted_iota(jnp.int32, (ROWS, LANES), 0).astype(F32)
    signal_ref[:, pl.ds(0, ROWS), :] = jnp.zeros((count, ROWS, LANES), F32)
    for tile in range(count):
        signal_ref[tile, pl.ds(ROWS, length), :] = mixed_ref[first + tile]

    def one_tile(tile, carry):
        starts, decay = [], []
        for mode in range(modes):
            rate = spread(mode_ref, first + tile, modes + mode)
            starts.append(spread(mode_ref, first + tile, mode) * jnp.exp(-rate * place))
            decay.append(jnp.exp(-rate * float(ROWS)))
        for at, value in enumerate(decayed_sums(starts, decay, blocks)):
            filter_ref[tile, pl.ds(ROWS * at, ROWS), :] = value
        sums = own_taps(signal_ref, filter_ref, tile, blocks)
        for at in range(blocks):
            conv_out[tile, pl.ds(ROWS * at, ROWS), :] = sums[at]
        return carry

    lax.fori_loop(0, count, one_tile, 0)


def first_local_kernel(mixed_ref, mode_ref, conv_out, signal_ref, filter_ref):
    local_conv(0, conv_out.shape[0], mixed_ref, mode_ref, conv_out, signal_ref, filter_ref)


def last_local_kernel(mixed_ref, mode_ref, one_ref, before_ref, conv_out, one_out, signal_ref, filter_ref):
    del before_ref
    count = conv_out.shape[0]
    local_conv(mixed_ref.shape[0] - count, count, mixed_ref, mode_ref, conv_out, signal_ref, filter_ref)
    for tile in range(one_ref.shape[0]):
        one_out[pl.ds(tile * LANES, LANES), :] = turned(one_ref[tile]).astype(BF16)


def near_kernel(heard_ref, mode_ref, conv_ref, before_out, whole_out):
    del conv_ref
    tiles, modes = mode_ref.shape[0], (mode_ref.shape[1] - ROWS) // 2
    chips = whole_out.shape[0]
    line, ring, core = lax.axis_index("line"), lax.axis_index("ring"), lax.axis_index("core")
    cores = lax.axis_size("core")
    ahead = (core * LANES).astype(F32)
    for tile in range(tiles):
        part = pl.ds(tile * modes, modes)
        rates = mode_ref[tile, pl.ds(modes, modes), :]
        step = jnp.exp(-rates * float(LANES))
        row = jnp.exp(-rates * float(LANES * cores * chips))
        lead = jnp.exp(-rates * ahead)
        zero = jnp.zeros((modes, LANES), F32)
        whole, earlier, upto, before = zero, zero, zero, zero
        for other in range(heard_ref.shape[0] // cores):
            chip = zero
            for peer in range(cores):
                chip = chip * step + heard_ref[other * cores + peer, part, :].astype(F32)
                before = jnp.where((other == line) & (peer < core), chip, before)
            whole = whole * row + chip * lead
            earlier = jnp.where(other < line, whole, earlier)
            upto = jnp.where(other == line, whole, upto)
        before_out[part, :] = before
        for peer in range(chips):
            whole_out[peer, part, :] = jnp.where(peer > ring, upto, earlier).astype(BF16)


def finish_kernel(heard_ref, before_ref, mode_ref, early_ref, late_ref, mixed_ref, gate_ref, out_ref):
    tiles, length = mixed_ref.shape[0], mixed_ref.shape[1]
    blocks = length // ROWS
    modes = (mode_ref.shape[1] - ROWS) // 2
    chips = heard_ref.shape[0]
    ring = lax.axis_index("ring")
    order = [lax.rem(ring + at, chips) for at in range(chips)]
    after = (1 + lax.broadcasted_iota(jnp.int32, (ROWS, LANES), 0)).astype(F32)
    for tile in range(tiles):
        part = pl.ds(tile * modes, modes)
        rates = mode_ref[tile, pl.ds(modes, modes), :]
        step = jnp.exp(-rates * float(length * lax.axis_size("core")))
        far = heard_ref[order[0], part, :].astype(F32)
        for peer in order[1:]:
            far = far * step + heard_ref[peer, part, :].astype(F32)
        entering = (before_ref[part, :] + far) * mode_ref[tile, pl.ds(0, modes), :]
        starts, decay = [], []
        for mode in range(modes):
            rate = jnp.broadcast_to(rates[mode : mode + 1, :], (ROWS, LANES))
            starts.append(jnp.broadcast_to(entering[mode : mode + 1, :], (ROWS, LANES)) * jnp.exp(-rate * after))
            decay.append(jnp.exp(-rate * float(ROWS)))
        gain = spread(mode_ref, tile, 2 * modes)
        early = early_ref.shape[0]
        conv_ref, at_tile = (early_ref, tile) if tile < early else (late_ref, tile - early)
        made = []
        for at, value in enumerate(decayed_sums(starts, decay, blocks)):
            rows = pl.ds(ROWS * at, ROWS)
            convolved = (conv_ref[at_tile, rows, :] + value).astype(BF16).astype(F32)
            made.append(convolved + gain * mixed_ref[tile, rows, :])
        channels = pl.ds(tile * LANES, LANES)
        summed = turned(jnp.concatenate(made, axis=0))
        out_ref[channels, :] = (gate_ref[channels, :].astype(F32) * summed).astype(BF16)


def body(q_one, k_one, v_one, fir_taps, q_two, k_two, residues, decays, skip_gain):
    channels, length = q_one.shape
    tiles, modes = channels // LANES, residues.shape[1]
    seq = ("line", "ring", "core")
    chips = lax.axis_size("ring")
    mates = lax.axis_size("line") * lax.axis_size("core")
    count = mates * chips
    wide = array(F32, tiles, length, LANES)
    states = tiles * modes
    product, mode_rows = call(
        product_kernel,
        (array(BF16, tiles, length, LANES), array(F32, tiles, 2 * modes + ROWS, LANES)),
    )(k_one, v_one, residues.T, decays.T, skip_gain.reshape(tiles, LANES))
    halo = lax.ppermute(product, seq, [(at, at + 1) for at in range(count - 1)])
    padded = pltpu.VMEM((tiles, length + ROWS, LANES), F32)
    taps, part = call(own_filter_kernel, (wide, wide), (padded,))(*near_by(product, fir_taps))
    q_turned, k_turned = call(turn_kernel, (wide, wide))(*near_by(q_one, k_two))
    one_turned, mixed, state = call(
        mix_kernel, (wide, wide, array(BF16, mates, states, LANES)), (padded,)
    )(*near_by(halo, part, taps, q_turned, k_turned, mode_rows))
    heard = lax.all_to_all(state, ("line", "core"), split_axis=0, concat_axis=0, tiled=True)
    early = tiles // 2
    held = array(F32, early, length, LANES)
    scratch = (pltpu.VMEM((early, length + ROWS, LANES), F32), pltpu.VMEM((early, length, LANES), F32))
    early_conv = call(first_local_kernel, held, scratch)(*near_by(mixed, mode_rows))
    before, whole = call(
        near_kernel, (array(F32, states, LANES), array(BF16, chips, states, LANES))
    )(*near_by(heard, mode_rows, early_conv))
    far_heard = lax.all_to_all(whole, "ring", split_axis=0, concat_axis=0, tiled=True)
    late_conv, layer_one = call(
        last_local_kernel, (held, jax.ShapeDtypeStruct((channels, length), BF16)), scratch
    )(*near_by(mixed, mode_rows, one_turned, before))
    layer_two = call(finish_kernel, jax.ShapeDtypeStruct((channels, length), BF16))(
        *near_by(far_heard, before, mode_rows, early_conv, late_conv, mixed, q_two)
    )
    return (layer_one, layer_two)


def solution(mesh):
    count, chans = mesh.shape["seq"], mesh.shape["chan"]
    split = (LINE, count // (LINE * CORES), CORES)
    grid = Mesh(mesh.devices.reshape(*split, chans), ("line", "ring", "core", "chan"))
    split = P("chan", ("line", "ring", "core"))
    whole = P("chan", None)
    return jax.shard_map(
        body,
        mesh=grid,
        in_specs=(split, split, split, whole, split, split, whole, whole, P("chan")),
        out_specs=(split, split),
        check_vma=False,
    )
```

```python
import jax
import jax.numpy as jnp
from jax import lax
from jax.experimental import pallas as pl
from jax.experimental.pallas import tpu as pltpu
from jax.sharding import Mesh, PartitionSpec as P

LANES = 128
ROWS = 8
F32 = jnp.float32
BF16 = jnp.bfloat16
LINE = 4
CORES = 2


def call(kernel, outs, scratch=()):
    return pl.pallas_call(kernel, out_shape=outs, scratch_shapes=list(scratch))


def near_by(*args):
    return [pltpu.with_memory_space_constraint(arg, pltpu.VMEM) for arg in args]


def array(dtype, *shape):
    return pltpu.VMEM(shape, dtype)


def turned(block):
    return jnp.swapaxes(block.astype(F32), 0, 1)


def rows_of(ref, tile, first, count=ROWS):
    return ref[tile, pl.ds(first, count), :]


def spread(ref, tile, row):
    return jnp.broadcast_to(ref[tile, pl.ds(row, 1), :], (ROWS, LANES))


def product_kernel(k_ref, v_ref, res_ref, dec_ref, gain_ref, out_ref, mode_out):
    modes = res_ref.shape[0]
    for tile in range(out_ref.shape[0]):
        part = pl.ds(tile * LANES, LANES)
        product = (k_ref[part, :].astype(F32) * v_ref[part, :].astype(F32)).astype(BF16)
        out_ref[tile] = turned(product).astype(BF16)
        mode_out[tile, pl.ds(0, modes), :] = res_ref[:, part]
        mode_out[tile, pl.ds(modes, modes), :] = dec_ref[:, part]
        mode_out[tile, pl.ds(2 * modes, 1), :] = gain_ref[pl.ds(tile, 1), :]


def own_taps(signal_ref, taps_ref, tile, blocks):
    sums = [jnp.zeros((ROWS, LANES), F32) for _ in range(blocks)]
    for offset in range(ROWS):
        shifted = [rows_of(signal_ref, tile, ROWS + ROWS * at - offset) for at in range(blocks)]
        for step in range(blocks):
            weight = spread(taps_ref, tile, ROWS * step + offset)
            for at in range(step, blocks):
                sums[at] = sums[at] + weight * shifted[at - step]
    return sums


def earlier_taps(sums, signal_ref, taps_ref, tile, blocks):
    def one_offset(offset, sums):
        sums = list(sums)
        shifted = [rows_of(signal_ref, tile, ROWS * (blocks - at) - offset) for at in range(blocks)]
        for step in range(blocks):
            weight = spread(taps_ref, tile, ROWS * step + offset)
            for at in range(step + 1):
                sums[at] = sums[at] + weight * shifted[step - at]
        return tuple(sums)

    return list(lax.fori_loop(0, ROWS, one_offset, tuple(sums)))


def decayed_sums(starts, decay, blocks):
    out = []
    for at in range(blocks):
        terms = list(starts)
        while len(terms) > 1:
            terms = [a + b for a, b in zip(terms[::2], terms[1::2])]
        out.append(terms[0])
        if at + 1 < blocks:
            starts = [a * b for a, b in zip(starts, decay)]
    return out


def own_filter_kernel(product_ref, taps_ref, taps_out, part_out, signal_ref):
    tiles, length = product_ref.shape[0], product_ref.shape[1]
    blocks = length // ROWS
    signal_ref[:, pl.ds(0, ROWS), :] = jnp.zeros((tiles, ROWS, LANES), F32)
    for tile in range(tiles):
        signal_ref[tile, pl.ds(ROWS, length), :] = product_ref[tile].astype(F32)
        taps_out[tile] = turned(taps_ref[pl.ds(tile * LANES, LANES), :])

    def one_tile(tile, carry):
        sums = own_taps(signal_ref, taps_out, tile, blocks)
        for at in range(blocks):
            part_out[tile, pl.ds(ROWS * at, ROWS), :] = sums[at]
        return carry

    lax.fori_loop(0, tiles, one_tile, 0)


def turn_kernel(q_ref, k_ref, q_out, k_out):
    for tile in range(q_out.shape[0]):
        part = pl.ds(tile * LANES, LANES)
        q_out[tile] = turned(q_ref[part, :])
        k_out[tile] = turned(k_ref[part, :])


def mix_kernel(
    halo_ref, part_ref, taps_ref, q_ref, k_ref, mode_ref,
    one_out, mixed_out, state_out,
    signal_ref,
):
    tiles, length = part_ref.shape[0], part_ref.shape[1]
    blocks = length // ROWS
    modes = state_out.shape[1] // tiles
    signal_ref[:, pl.ds(length, ROWS), :] = jnp.zeros((tiles, ROWS, LANES), F32)
    for tile in range(tiles):
        signal_ref[tile, pl.ds(0, length), :] = halo_ref[tile].astype(F32)

    left = (ROWS - 1 - lax.broadcasted_iota(jnp.int32, (ROWS, LANES), 0)).astype(F32)

    def one_tile(tile, carry):
        sums = [rows_of(part_ref, tile, ROWS * at) for at in range(blocks)]
        sums = earlier_taps(sums, signal_ref, taps_ref, tile, blocks)
        mixed = []
        for at in range(blocks):
            rows = pl.ds(ROWS * at, ROWS)
            first = (q_ref[tile, rows, :] * sums[at]).astype(BF16).astype(F32)
            mixed.append((k_ref[tile, rows, :] * first).astype(BF16).astype(F32))
            one_out[tile, rows, :] = first
            mixed_out[tile, rows, :] = mixed[-1]
        found = []
        for mode in range(modes):
            rate = spread(mode_ref, tile, modes + mode)
            decay = jnp.exp(-rate * float(ROWS))
            held = mixed[0]
            for at in range(1, blocks):
                held = held * decay + mixed[at]
            found.append(jnp.sum(held * jnp.exp(-rate * left), axis=0, keepdims=True))
        state = jnp.concatenate(found, axis=0).astype(BF16)
        for peer in range(state_out.shape[0]):
            state_out[peer, pl.ds(pl.multiple_of(tile * modes, modes), modes), :] = state
        return carry

    lax.fori_loop(0, tiles, one_tile, 0)


def local_conv(first, count, mixed_ref, mode_ref, conv_out, signal_ref, filter_ref):
    length = mixed_ref.shape[1]
    blocks = length // ROWS
    modes = (mode_ref.shape[1] - ROWS) // 2
    place = lax.broadcasted_iota(jnp.int32, (ROWS, LANES), 0).astype(F32)
    signal_ref[:, pl.ds(0, ROWS), :] = jnp.zeros((count, ROWS, LANES), F32)
    for tile in range(count):
        signal_ref[tile, pl.ds(ROWS, length), :] = mixed_ref[first + tile]

    def one_tile(tile, carry):
        starts, decay = [], []
        for mode in range(modes):
            rate = spread(mode_ref, first + tile, modes + mode)
            starts.append(spread(mode_ref, first + tile, mode) * jnp.exp(-rate * place))
            decay.append(jnp.exp(-rate * float(ROWS)))
        for at, value in enumerate(decayed_sums(starts, decay, blocks)):
            filter_ref[tile, pl.ds(ROWS * at, ROWS), :] = value
        sums = own_taps(signal_ref, filter_ref, tile, blocks)
        for at in range(blocks):
            conv_out[tile, pl.ds(ROWS * at, ROWS), :] = sums[at]
        return carry

    lax.fori_loop(0, count, one_tile, 0)


def first_local_kernel(mixed_ref, mode_ref, conv_out, signal_ref, filter_ref):
    local_conv(0, conv_out.shape[0], mixed_ref, mode_ref, conv_out, signal_ref, filter_ref)


def early_after_kernel(mixed_ref, mode_ref, before_ref, conv_out, signal_ref, filter_ref):
    local_conv(0, conv_out.shape[0], mixed_ref, mode_ref, conv_out, signal_ref, filter_ref)


def last_local_kernel(mixed_ref, mode_ref, one_ref, before_ref, conv_out, one_out, signal_ref, filter_ref):
    del before_ref
    count = conv_out.shape[0]
    local_conv(mixed_ref.shape[0] - count, count, mixed_ref, mode_ref, conv_out, signal_ref, filter_ref)
    for tile in range(one_ref.shape[0]):
        one_out[pl.ds(tile * LANES, LANES), :] = turned(one_ref[tile]).astype(BF16)


def near_kernel(heard_ref, mode_ref, conv_ref, before_out, whole_out):
    del conv_ref
    tiles, modes = mode_ref.shape[0], (mode_ref.shape[1] - ROWS) // 2
    chips = whole_out.shape[0]
    line, ring, core = lax.axis_index("line"), lax.axis_index("ring"), lax.axis_index("core")
    cores = lax.axis_size("core")
    ahead = (core * LANES).astype(F32)
    for tile in range(tiles):
        part = pl.ds(tile * modes, modes)
        rates = mode_ref[tile, pl.ds(modes, modes), :]
        step = jnp.exp(-rates * float(LANES))
        row = jnp.exp(-rates * float(LANES * cores * chips))
        lead = jnp.exp(-rates * ahead)
        zero = jnp.zeros((modes, LANES), F32)
        whole, earlier, upto, before = zero, zero, zero, zero
        for other in range(heard_ref.shape[0] // cores):
            chip = zero
            for peer in range(cores):
                chip = chip * step + heard_ref[other * cores + peer, part, :].astype(F32)
                before = jnp.where((other == line) & (peer < core), chip, before)
            whole = whole * row + chip * lead
            earlier = jnp.where(other < line, whole, earlier)
            upto = jnp.where(other == line, whole, upto)
        before_out[part, :] = before
        for peer in range(chips):
            whole_out[peer, part, :] = jnp.where(peer > ring, upto, earlier).astype(BF16)


def finish_kernel(heard_ref, before_ref, mode_ref, early_ref, late_ref, mixed_ref, gate_ref, out_ref):
    tiles, length = mixed_ref.shape[0], mixed_ref.shape[1]
    blocks = length // ROWS
    modes = (mode_ref.shape[1] - ROWS) // 2
    chips = heard_ref.shape[0]
    ring = lax.axis_index("ring")
    order = [lax.rem(ring + at, chips) for at in range(chips)]
    after = (1 + lax.broadcasted_iota(jnp.int32, (ROWS, LANES), 0)).astype(F32)
    for tile in range(tiles):
        part = pl.ds(tile * modes, modes)
        rates = mode_ref[tile, pl.ds(modes, modes), :]
        step = jnp.exp(-rates * float(length * lax.axis_size("core")))
        far = heard_ref[order[0], part, :].astype(F32)
        for peer in order[1:]:
            far = far * step + heard_ref[peer, part, :].astype(F32)
        entering = (before_ref[part, :] + far) * mode_ref[tile, pl.ds(0, modes), :]
        starts, decay = [], []
        for mode in range(modes):
            rate = jnp.broadcast_to(rates[mode : mode + 1, :], (ROWS, LANES))
            starts.append(jnp.broadcast_to(entering[mode : mode + 1, :], (ROWS, LANES)) * jnp.exp(-rate * after))
            decay.append(jnp.exp(-rate * float(ROWS)))
        gain = spread(mode_ref, tile, 2 * modes)
        early = early_ref.shape[0]
        conv_ref, at_tile = (early_ref, tile) if tile < early else (late_ref, tile - early)
        made = []
        for at, value in enumerate(decayed_sums(starts, decay, blocks)):
            rows = pl.ds(ROWS * at, ROWS)
            convolved = (conv_ref[at_tile, rows, :] + value).astype(BF16).astype(F32)
            made.append(convolved + gain * mixed_ref[tile, rows, :])
        channels = pl.ds(tile * LANES, LANES)
        summed = turned(jnp.concatenate(made, axis=0))
        out_ref[channels, :] = (gate_ref[channels, :].astype(F32) * summed).astype(BF16)


def body(q_one, k_one, v_one, fir_taps, q_two, k_two, residues, decays, skip_gain):
    channels, length = q_one.shape
    tiles, modes = channels // LANES, residues.shape[1]
    seq = ("line", "ring", "core")
    chips = lax.axis_size("ring")
    mates = lax.axis_size("line") * lax.axis_size("core")
    count = mates * chips
    wide = array(F32, tiles, length, LANES)
    states = tiles * modes
    product, mode_rows = call(
        product_kernel,
        (array(BF16, tiles, length, LANES), array(F32, tiles, 2 * modes + ROWS, LANES)),
    )(k_one, v_one, residues.T, decays.T, skip_gain.reshape(tiles, LANES))
    halo = lax.ppermute(product, seq, [(at, at + 1) for at in range(count - 1)])
    padded = pltpu.VMEM((tiles, length + ROWS, LANES), F32)
    taps, part = call(own_filter_kernel, (wide, wide), (padded,))(*near_by(product, fir_taps))
    q_turned, k_turned = call(turn_kernel, (wide, wide))(*near_by(q_one, k_two))
    one_turned, mixed, state = call(
        mix_kernel, (wide, wide, array(BF16, mates, states, LANES)), (padded,)
    )(*near_by(halo, part, taps, q_turned, k_turned, mode_rows))
    heard = lax.all_to_all(state, ("line", "core"), split_axis=0, concat_axis=0, tiled=True)
    early = tiles // 2
    held = array(F32, early, length, LANES)
    scratch = (pltpu.VMEM((early, length + ROWS, LANES), F32), pltpu.VMEM((early, length, LANES), F32))
    before, whole = call(
        near_kernel, (array(F32, states, LANES), array(BF16, chips, states, LANES))
    )(*near_by(heard, mode_rows, mode_rows))
    far_heard = lax.all_to_all(whole, "ring", split_axis=0, concat_axis=0, tiled=True)
    early_conv = call(early_after_kernel, held, scratch)(*near_by(mixed, mode_rows, before))
    late_conv, layer_one = call(
        last_local_kernel, (held, jax.ShapeDtypeStruct((channels, length), BF16)), scratch
    )(*near_by(mixed, mode_rows, one_turned, before))
    layer_two = call(finish_kernel, jax.ShapeDtypeStruct((channels, length), BF16))(
        *near_by(far_heard, before, mode_rows, early_conv, late_conv, mixed, q_two)
    )
    return (layer_one, layer_two)


def solution(mesh):
    count, chans = mesh.shape["seq"], mesh.shape["chan"]
    split = (LINE, count // (LINE * CORES), CORES)
    grid = Mesh(mesh.devices.reshape(*split, chans), ("line", "ring", "core", "chan"))
    split = P("chan", ("line", "ring", "core"))
    whole = P("chan", None)
    return jax.shard_map(
        body,
        mesh=grid,
        in_specs=(split, split, split, whole, split, split, whole, whole, P("chan")),
        out_specs=(split, split),
        check_vma=False,
    )
```

```python
import jax
import jax.numpy as jnp
import numpy as np
from jax import lax
from jax.experimental import pallas as pl
from jax.experimental.pallas import tpu as pltpu
from jax.sharding import Mesh, PartitionSpec as P

LANES = 128
ROWS = 8
F32 = jnp.float32
BF16 = jnp.bfloat16
LINE = 4
CORES = 2


def call(kernel, outs, scratch=()):
    limit = pltpu.CompilerParams(vmem_limit_bytes=16 << 20)
    return pl.pallas_call(kernel, out_shape=outs, scratch_shapes=list(scratch), compiler_params=limit)


def near_by(*args):
    return [pltpu.with_memory_space_constraint(arg, pltpu.VMEM) for arg in args]


def array(dtype, *shape):
    return pltpu.VMEM(shape, dtype)


def turned(block):
    return jnp.swapaxes(block.astype(F32), 0, 1)


def rows_of(ref, tile, first, count=ROWS):
    return ref[tile, pl.ds(first, count), :]


def spread(ref, tile, row):
    return jnp.broadcast_to(ref[tile, pl.ds(row, 1), :], (ROWS, LANES))


def product_kernel(k_ref, v_ref, res_ref, dec_ref, gain_ref, out_ref, mode_out):
    modes = res_ref.shape[0]
    for tile in range(out_ref.shape[0]):
        part = pl.ds(tile * LANES, LANES)
        product = (k_ref[part, :].astype(F32) * v_ref[part, :].astype(F32)).astype(BF16)
        out_ref[tile] = turned(product).astype(BF16)
        mode_out[tile, pl.ds(0, modes), :] = res_ref[:, part]
        mode_out[tile, pl.ds(modes, modes), :] = dec_ref[:, part]
        mode_out[tile, pl.ds(2 * modes, 1), :] = gain_ref[pl.ds(tile, 1), :]


def own_taps(signal_ref, taps_ref, tile, blocks):
    sums = [jnp.zeros((ROWS, LANES), F32) for _ in range(blocks)]
    for offset in range(ROWS):
        shifted = [rows_of(signal_ref, tile, ROWS + ROWS * at - offset) for at in range(blocks)]
        for step in range(blocks):
            weight = spread(taps_ref, tile, ROWS * step + offset)
            for at in range(step, blocks):
                sums[at] = sums[at] + weight * shifted[at - step]
    return sums


def spectrum_tables(length):
    points = 2 * length
    angle = 2.0 * np.pi / points * (np.arange(length)[:, None] * np.arange(points)[None, :] % points)
    real, imag = np.cos(angle), -np.sin(angle)
    imag[0] = np.cos(np.pi * np.arange(points))
    there = np.concatenate([real, imag])[:, :length]
    weight = np.full((2 * length, 1), 2.0 / points)
    weight[0] = weight[length] = 1.0 / points
    back = (np.concatenate([real, imag]) * weight)[:, length:].T

    def parts(table):
        table = table.astype(np.float32)
        high = table.astype(jnp.bfloat16)
        return np.concatenate([high, (table - high.astype(np.float32)).astype(jnp.bfloat16)])

    return parts(there), parts(back)


def times(table, values):
    both = jnp.dot(table, values, preferred_element_type=F32)
    half = both.shape[0] // 2
    return both[:half] + both[half:]


def side_by_side(ref):
    return jnp.concatenate([ref[tile].astype(BF16) for tile in range(ref.shape[0])], axis=1)


def decayed_sums(starts, decay, blocks):
    out = []
    for at in range(blocks):
        terms = list(starts)
        while len(terms) > 1:
            terms = [a + b for a, b in zip(terms[::2], terms[1::2])]
        out.append(terms[0])
        if at + 1 < blocks:
            starts = [a * b for a, b in zip(starts, decay)]
    return out


def own_filter_kernel(product_ref, taps_ref, there_ref, wave_out, part_out, signal_ref, taps_out):
    tiles, length = product_ref.shape[0], product_ref.shape[1]
    blocks = length // ROWS
    signal_ref[:, pl.ds(0, ROWS), :] = jnp.zeros((tiles, ROWS, LANES), F32)
    for tile in range(tiles):
        signal_ref[tile, pl.ds(ROWS, length), :] = product_ref[tile].astype(F32)
        taps_out[tile] = turned(taps_ref[pl.ds(tile * LANES, LANES), :])
    wave = times(there_ref[...], side_by_side(taps_out))
    real, imag = wave[:length], wave[length:]
    top = lax.broadcasted_iota(jnp.int32, real.shape, 0) == 0
    wave_out[0] = real
    wave_out[1] = jnp.where(top, 0.0, imag)
    wave_out[2] = jnp.where(top, imag, real)

    def one_tile(tile, carry):
        sums = own_taps(signal_ref, taps_out, tile, blocks)
        for at in range(blocks):
            part_out[tile, pl.ds(ROWS * at, ROWS), :] = sums[at]
        return carry

    lax.fori_loop(0, tiles, one_tile, 0)


def turn_kernel(q_ref, k_ref, q_out, k_out):
    for tile in range(q_out.shape[0]):
        part = pl.ds(tile * LANES, LANES)
        q_out[tile] = turned(q_ref[part, :])
        k_out[tile] = turned(k_ref[part, :])


def mix_kernel(
    halo_ref, part_ref, wave_ref, there_ref, back_ref, q_ref, k_ref, mode_ref,
    one_out, mixed_out, state_out,
    earlier_ref,
):
    tiles, length = part_ref.shape[0], part_ref.shape[1]
    blocks = length // ROWS
    modes = state_out.shape[1] // tiles
    wave = times(there_ref[...], side_by_side(halo_ref))
    real, imag = wave[:length], wave[length:]
    made = jnp.concatenate(
        [real * wave_ref[0] - imag * wave_ref[1], real * wave_ref[1] + imag * wave_ref[2]], axis=0
    )
    high = made.astype(BF16)
    low = (made - high.astype(F32)).astype(BF16)
    earlier_ref[...] = times(back_ref[...], high) + jnp.dot(
        back_ref[pl.ds(0, length), :], low, preferred_element_type=F32
    )

    left = (ROWS - 1 - lax.broadcasted_iota(jnp.int32, (ROWS, LANES), 0)).astype(F32)

    for tile in range(tiles):
        mixed = []
        for at in range(blocks):
            rows = pl.ds(ROWS * at, ROWS)
            summed = part_ref[tile, rows, :] + earlier_ref[rows, pl.ds(tile * LANES, LANES)]
            first = (q_ref[tile, rows, :] * summed).astype(BF16).astype(F32)
            mixed.append((k_ref[tile, rows, :] * first).astype(BF16).astype(F32))
            one_out[tile, rows, :] = first
            mixed_out[tile, rows, :] = mixed[-1]
        found = []
        for mode in range(modes):
            rate = spread(mode_ref, tile, modes + mode)
            decay = jnp.exp(-rate * float(ROWS))
            held = mixed[0]
            for at in range(1, blocks):
                held = held * decay + mixed[at]
            found.append(jnp.sum(held * jnp.exp(-rate * left), axis=0, keepdims=True))
        state = jnp.concatenate(found, axis=0).astype(BF16)
        for peer in range(state_out.shape[0]):
            state_out[peer, pl.ds(tile * modes, modes), :] = state


def local_conv(first, count, mixed_ref, mode_ref, conv_out, signal_ref, filter_ref):
    length = mixed_ref.shape[1]
    blocks = length // ROWS
    modes = (mode_ref.shape[1] - ROWS) // 2
    place = lax.broadcasted_iota(jnp.int32, (ROWS, LANES), 0).astype(F32)
    signal_ref[:, pl.ds(0, ROWS), :] = jnp.zeros((count, ROWS, LANES), F32)
    for tile in range(count):
        signal_ref[tile, pl.ds(ROWS, length), :] = mixed_ref[first + tile]

    def one_tile(tile, carry):
        starts, decay = [], []
        for mode in range(modes):
            rate = spread(mode_ref, first + tile, modes + mode)
            starts.append(spread(mode_ref, first + tile, mode) * jnp.exp(-rate * place))
            decay.append(jnp.exp(-rate * float(ROWS)))
        for at, value in enumerate(decayed_sums(starts, decay, blocks)):
            filter_ref[tile, pl.ds(ROWS * at, ROWS), :] = value
        sums = own_taps(signal_ref, filter_ref, tile, blocks)
        for at in range(blocks):
            conv_out[tile, pl.ds(ROWS * at, ROWS), :] = sums[at]
        return carry

    lax.fori_loop(0, count, one_tile, 0)


def first_local_kernel(mixed_ref, mode_ref, conv_out, signal_ref, filter_ref):
    local_conv(0, conv_out.shape[0], mixed_ref, mode_ref, conv_out, signal_ref, filter_ref)


def early_after_kernel(mixed_ref, mode_ref, before_ref, conv_out, signal_ref, filter_ref):
    local_conv(0, conv_out.shape[0], mixed_ref, mode_ref, conv_out, signal_ref, filter_ref)


def last_local_kernel(mixed_ref, mode_ref, one_ref, before_ref, conv_out, one_out, signal_ref, filter_ref):
    del before_ref
    count = conv_out.shape[0]
    local_conv(mixed_ref.shape[0] - count, count, mixed_ref, mode_ref, conv_out, signal_ref, filter_ref)
    for tile in range(one_ref.shape[0]):
        one_out[pl.ds(tile * LANES, LANES), :] = turned(one_ref[tile]).astype(BF16)


def near_kernel(heard_ref, mode_ref, conv_ref, before_out, whole_out):
    del conv_ref
    tiles, modes = mode_ref.shape[0], (mode_ref.shape[1] - ROWS) // 2
    chips = whole_out.shape[0]
    line, ring, core = lax.axis_index("line"), lax.axis_index("ring"), lax.axis_index("core")
    cores = lax.axis_size("core")
    ahead = (core * LANES).astype(F32)
    for tile in range(tiles):
        part = pl.ds(tile * modes, modes)
        rates = mode_ref[tile, pl.ds(modes, modes), :]
        step = jnp.exp(-rates * float(LANES))
        row = jnp.exp(-rates * float(LANES * cores * chips))
        lead = jnp.exp(-rates * ahead)
        zero = jnp.zeros((modes, LANES), F32)
        whole, earlier, upto, before = zero, zero, zero, zero
        for other in range(heard_ref.shape[0] // cores):
            chip = zero
            for peer in range(cores):
                chip = chip * step + heard_ref[other * cores + peer, part, :].astype(F32)
                before = jnp.where((other == line) & (peer < core), chip, before)
            whole = whole * row + chip * lead
            earlier = jnp.where(other < line, whole, earlier)
            upto = jnp.where(other == line, whole, upto)
        before_out[part, :] = before
        for peer in range(chips):
            whole_out[peer, part, :] = jnp.where(peer > ring, upto, earlier).astype(BF16)


def finish_kernel(heard_ref, before_ref, mode_ref, early_ref, late_ref, mixed_ref, gate_ref, out_ref):
    tiles, length = mixed_ref.shape[0], mixed_ref.shape[1]
    blocks = length // ROWS
    modes = (mode_ref.shape[1] - ROWS) // 2
    chips = heard_ref.shape[0]
    ring = lax.axis_index("ring")
    order = [lax.rem(ring + at, chips) for at in range(chips)]
    after = (1 + lax.broadcasted_iota(jnp.int32, (ROWS, LANES), 0)).astype(F32)
    for tile in range(tiles):
        part = pl.ds(tile * modes, modes)
        rates = mode_ref[tile, pl.ds(modes, modes), :]
        step = jnp.exp(-rates * float(length * lax.axis_size("core")))
        far = heard_ref[order[0], part, :].astype(F32)
        for peer in order[1:]:
            far = far * step + heard_ref[peer, part, :].astype(F32)
        entering = (before_ref[part, :] + far) * mode_ref[tile, pl.ds(0, modes), :]
        starts, decay = [], []
        for mode in range(modes):
            rate = jnp.broadcast_to(rates[mode : mode + 1, :], (ROWS, LANES))
            starts.append(jnp.broadcast_to(entering[mode : mode + 1, :], (ROWS, LANES)) * jnp.exp(-rate * after))
            decay.append(jnp.exp(-rate * float(ROWS)))
        gain = spread(mode_ref, tile, 2 * modes)
        early = early_ref.shape[0]
        conv_ref, at_tile = (early_ref, tile) if tile < early else (late_ref, tile - early)
        made = []
        for at, value in enumerate(decayed_sums(starts, decay, blocks)):
            rows = pl.ds(ROWS * at, ROWS)
            convolved = (conv_ref[at_tile, rows, :] + value).astype(BF16).astype(F32)
            made.append(convolved + gain * mixed_ref[tile, rows, :])
        channels = pl.ds(tile * LANES, LANES)
        summed = turned(jnp.concatenate(made, axis=0))
        out_ref[channels, :] = (gate_ref[channels, :].astype(F32) * summed).astype(BF16)


def body(q_one, k_one, v_one, fir_taps, q_two, k_two, residues, decays, skip_gain):
    channels, length = q_one.shape
    tiles, modes = channels // LANES, residues.shape[1]
    seq = ("line", "ring", "core")
    chips = lax.axis_size("ring")
    mates = lax.axis_size("line") * lax.axis_size("core")
    count = mates * chips
    wide = array(F32, tiles, length, LANES)
    states = tiles * modes
    product, mode_rows = call(
        product_kernel,
        (array(BF16, tiles, length, LANES), array(F32, tiles, 2 * modes + ROWS, LANES)),
    )(k_one, v_one, residues.T, decays.T, skip_gain.reshape(tiles, LANES))
    halo = lax.ppermute(product, seq, [(at, at + 1) for at in range(count - 1)])
    padded = pltpu.VMEM((tiles, length + ROWS, LANES), F32)
    there, back = (jnp.asarray(table) for table in spectrum_tables(length))
    waves = array(F32, 3, length, channels)
    wave, part = call(own_filter_kernel, (waves, wide), (padded, pltpu.VMEM((tiles, length, LANES), F32)))(
        *near_by(product, fir_taps, there)
    )
    q_turned, k_turned = call(turn_kernel, (wide, wide))(*near_by(q_one, k_two))
    one_turned, mixed, state = call(
        mix_kernel, (wide, wide, array(BF16, mates, states, LANES)),
        (pltpu.VMEM((length, channels), F32),),
    )(*near_by(halo, part, wave, there, back, q_turned, k_turned, mode_rows))
    heard = lax.all_to_all(state, ("line", "core"), split_axis=0, concat_axis=0, tiled=True)
    early = tiles // 2
    held = array(F32, early, length, LANES)
    scratch = (pltpu.VMEM((early, length + ROWS, LANES), F32), pltpu.VMEM((early, length, LANES), F32))
    before, whole = call(
        near_kernel, (array(F32, states, LANES), array(BF16, chips, states, LANES))
    )(*near_by(heard, mode_rows, mode_rows))
    far_heard = lax.all_to_all(whole, "ring", split_axis=0, concat_axis=0, tiled=True)
    early_conv = call(early_after_kernel, held, scratch)(*near_by(mixed, mode_rows, before))
    late_conv, layer_one = call(
        last_local_kernel, (held, jax.ShapeDtypeStruct((channels, length), BF16)), scratch
    )(*near_by(mixed, mode_rows, one_turned, before))
    layer_two = call(finish_kernel, jax.ShapeDtypeStruct((channels, length), BF16))(
        *near_by(far_heard, before, mode_rows, early_conv, late_conv, mixed, q_two)
    )
    return (layer_one, layer_two)


def solution(mesh):
    count, chans = mesh.shape["seq"], mesh.shape["chan"]
    split = (LINE, count // (LINE * CORES), CORES)
    grid = Mesh(mesh.devices.reshape(*split, chans), ("line", "ring", "core", "chan"))
    split = P("chan", ("line", "ring", "core"))
    whole = P("chan", None)
    return jax.shard_map(
        body,
        mesh=grid,
        in_specs=(split, split, split, whole, split, split, whole, whole, P("chan")),
        out_specs=(split, split),
        check_vma=False,
    )
```
